32 devices in a mesh: groups: 2 (over x), frame: 8 (over z, y), band: 2 (over core).
Axes of the slice: x: 2, y: 2, z: 4, core: 2. Of those that a mesh axis runs over, the one named last changes fastest.
Arguments:
- hidden_in: bfloat16 [16, 1536, 1152], P(('groups', 'frame'), 'band'), parts along dimension 0, may hold values from -6 to 6
- latents: float32 [16, 192, 128], P(('groups', 'frame'), 'band'), parts along dimension 0, may hold values from -6 to 6
- fresh_noise: float32 [384, 128], P(('groups', 'band')), parts along dimension 0, may hold values from -6 to 6
- level_index: int32 [16], P(('groups', 'frame')), parts along dimension 0, may hold values from 1 to 31
- time_table: int32 [32], replicated, may hold values from 0 to 999, as said below
- frame_offset: int32 [2], P('groups'), parts along dimension 0, may hold values from 0 to 1023
- mod_table: float32 [3456], replicated, may hold values from -3 to 3
- time_weight: bfloat16 [128, 3456], replicated, may hold values from -0.5 to 0.5
- spatial_qkv: bfloat16 [1152, 1728], replicated, may hold values from -6 to 6
- spatial_out: bfloat16 [576, 1152], replicated, may hold values from -0.25 to 0.25
- temporal_qkv: bfloat16 [1152, 1728], replicated, may hold values from -6 to 6
- temporal_out: bfloat16 [576, 1152], replicated, may hold values from -0.25 to 0.25
- final_gain: float32 [1152], replicated, may hold values from 0.5 to 1.5
- out_weight: bfloat16 [1152, 16], replicated, may hold values from -0.1875 to 0.1875
Outputs:
- hidden_out: bfloat16 [16, 1536, 1152], P(('groups', 'frame'), 'band'), parts along dimension 0
- velocity: float32 [16, 192, 128], P(('groups', 'frame'), 'band'), parts along dimension 0
- next_latents: float32 [16, 192, 128], P(('groups', 'frame'), 'band'), parts along dimension 0
The draws below stay inside these ranges and needn't reach their ends.
There are 2 independent parts, one for each index of `groups`. The reference program is written for one: setup_inputs(seed, part) draws one part's arguments, and reference() takes and returns one part's arrays. A program takes and returns all parts, laid end to end along the dimension named above; an argument that names none is the same for every part. Nothing has to cross between parts.
Inputs may be any that keep to these rules, and one draw needn't show every extreme that they name: `time_table`: entries rise strictly along the table, from 0 at the first entry to 999 at the last.
All inputs are finite; a program needn't handle non-finite values.
Results may differ from the reference program's by a relative error of at most 0.025.
Values may be sent and summed in bfloat16 or wider, within the bound.
A program may use at most 128 MiB of HBM per device.

```python
import math
import jax
import jax.numpy as jnp
from jax import lax

D = 1152
HEADS = 8
HEAD_SIZE = 72
TFREQ = 128
LCH = 16
FT = 1536
FRAMES = 8
TLEN = 32


def draw_time_table(key, part):
    chosen = jax.random.permutation(jax.random.fold_in(key, 11), 998)[:TLEN - 2] + 1
    middle = jnp.sort(chosen.astype(jnp.int32))
    return jnp.concatenate([jnp.zeros((1,), jnp.int32), middle, jnp.full((1,), 999, jnp.int32)])


def drawn_weight(key, salt):
    base = jax.random.normal(jax.random.fold_in(key, salt), (D, 3, HEADS, HEAD_SIZE), jnp.float32)
    base = jnp.clip(base, -6.0, 6.0) / math.sqrt(D)
    return base.reshape(D, 3 * HEADS * HEAD_SIZE).astype(jnp.bfloat16)


def draw_spatial_qkv(key, part):
    return drawn_weight(key, 21)


def draw_temporal_qkv(key, part):
    return drawn_weight(key, 37)


def draw_hidden_in(key, part):
    values = jnp.clip(jax.random.normal(jax.random.fold_in(key, 51), (FRAMES, FT, D), jnp.float32), -6.0, 6.0)
    return values.astype(jnp.bfloat16)


def set_ends(entries, own_key, least, high):
    longest = entries.shape.index(max(entries.shape))
    spots = []
    for shift in (0, 1):
        where = [jax.random.randint(jax.random.fold_in(own_key, axis), (), 0, length) for axis, length in enumerate(entries.shape)]
        where[longest] = (where[longest] + shift) % entries.shape[longest]
        spots.append(tuple(where))
    return entries.at[spots[0]].set(least).at[spots[1]].set(high)


def block_levels(rng, dims, shards, smallest, largest):
    def one(dim, parts):
        heights = jax.random.uniform(jax.random.fold_in(jax.random.fold_in(rng, 6), dim), (parts,), jnp.float32, smallest / len(shards), largest / len(shards))
        return jnp.repeat(jnp.exp(heights), dims[dim] // parts).reshape((-1,) + (1,) * (len(dims) - dim - 1))

    gain = one(*shards[0])
    for cut in shards[1:]:
        gain = gain * one(*cut)
    return gain


def scatter_about(stream_key, extent, deviation, reach, split=(), held_as=jnp.bfloat16):
    gain = block_levels(stream_key, extent, split, -0.22, 0.18) if split else 1.0
    result = jax.random.normal(stream_key, extent, jnp.float32) * deviation * gain
    return jnp.minimum(jnp.maximum(result, -reach), reach).astype(held_as)


def setup_inputs(seed: int = 0, part: int = 0) -> dict:
    splits = jax.random.split(jax.random.key(seed), 15)
    part_keys = jax.random.split(jax.random.fold_in(splits[14], part), 15)
    return {
        "hidden_in": draw_hidden_in(jax.random.fold_in(jax.random.fold_in(splits[14], part), 71), part),
        "latents": scatter_about(part_keys[1], (FRAMES, FT * LCH // 128, 128), 1.0, 6.0, ((0, 8), (1, 2)), jnp.float32),
        "fresh_noise": scatter_about(part_keys[2], (FT * LCH // 128, 128), 1.0, 6.0, ((0, 2),), jnp.float32),
        "level_index": set_ends(jax.random.randint(part_keys[3], (FRAMES,), 1, TLEN), jax.random.fold_in(part_keys[3], 1), 1, TLEN - 1).astype(jnp.int32),
        "time_table": draw_time_table(jax.random.fold_in(splits[14], 71), part),
        "frame_offset": jax.random.randint(part_keys[5], (1,), 0, 1024).astype(jnp.int32),
        "mod_table": scatter_about(splits[6], (3 * D,), 0.5, 3.0, (), jnp.float32),
        "time_weight": scatter_about(splits[7], (TFREQ, 3 * D), TFREQ ** -0.5, 0.5),
        "spatial_qkv": draw_spatial_qkv(jax.random.fold_in(splits[14], 71), part),
        "spatial_out": scatter_about(splits[9], (HEADS * HEAD_SIZE, D), (HEADS * HEAD_SIZE) ** -0.5, 0.25),
        "temporal_qkv": draw_temporal_qkv(jax.random.fold_in(splits[14], 71), part),
        "temporal_out": scatter_about(splits[11], (HEADS * HEAD_SIZE, D), (HEADS * HEAD_SIZE) ** -0.5, 0.25),
        "final_gain": jnp.clip(1.0 + 0.1 * jax.random.normal(splits[12], (D,), jnp.float32), 0.5, 1.5),
        "out_weight": scatter_about(splits[13], (D, LCH), D ** -0.5, 0.1875),
    }


epsilon = 1e-06

def layer_norm(values):
    average = lax.optimization_barrier(jnp.mean(values, axis=-1, keepdims=True))
    centred = values - average
    variance = lax.optimization_barrier(jnp.mean(centred * centred, axis=-1, keepdims=True))
    return centred * lax.rsqrt(variance + epsilon)

def sinusoid(position, feature_count, first_sine):
    half_width = feature_count // 2
    frequency = jnp.exp(-math.log(10000.0) * jnp.arange(half_width, dtype=jnp.float32) / half_width)
    angles = position.astype(jnp.float32)[:, None] * frequency[None, :]
    if first_sine:
        return jnp.concatenate([jnp.sin(angles), jnp.cos(angles)], axis=-1)
    return jnp.concatenate([jnp.cos(angles), jnp.sin(angles)], axis=-1)

def attend(query_rows, key_matrix_rows, value_matrix_rows):
    attention_scores = jnp.einsum('ubg,wbg->buw', query_rows.astype(jnp.float32), key_matrix_rows.astype(jnp.float32)) / math.sqrt(HEAD_SIZE)
    row_max = lax.optimization_barrier(jnp.max(attention_scores, axis=-1, keepdims=True))
    attention_weight = jnp.exp(attention_scores - row_max).astype(jnp.bfloat16)
    denominator = lax.optimization_barrier(jnp.sum(attention_weight.astype(jnp.float32), axis=-1))
    weighted_sum = jnp.einsum('leq,qlr->ler', attention_weight.astype(jnp.float32), value_matrix_rows.astype(jnp.float32))
    mixed = weighted_sum / denominator[:, :, None]
    return jnp.transpose(mixed, (1, 0, 2)).reshape(query_rows.shape[0], -1).astype(jnp.bfloat16)

def reference(hidden_in, latents, fresh_noise, level_index, time_table, frame_offset, mod_table, time_weight, spatial_qkv, spatial_out, temporal_qkv, temporal_out, final_gain, out_weight):
    frames, frame_tokens, model_width = hidden_in.shape
    attended = spatial_out.shape[0]
    head_count = attended // HEAD_SIZE
    now_steps = time_table[level_index]
    next_steps = time_table[level_index - 1]
    activated = jax.nn.silu(sinusoid(now_steps, TFREQ, False)).astype(jnp.bfloat16)
    modulation = mod_table[None, :] + jnp.dot(activated, time_weight, preferred_element_type=jnp.float32)
    shift_part = modulation[:, None, :model_width]
    scale_part = modulation[:, None, model_width:2 * model_width]
    gate_part = modulation[:, None, 2 * model_width:]
    inputs = hidden_in.astype(jnp.float32)
    normed = (layer_norm(inputs) * (1.0 + scale_part) + shift_part).astype(jnp.bfloat16)

    def spatial_frame(frame_rows):
        projected = jnp.dot(frame_rows, spatial_qkv, preferred_element_type=jnp.float32).astype(jnp.bfloat16)
        parted = projected.reshape(frame_tokens, 3, head_count, HEAD_SIZE)
        mixed = attend(parted[:, 0], parted[:, 1], parted[:, 2])
        return jnp.dot(mixed, spatial_out, preferred_element_type=jnp.float32)
    residual = inputs + gate_part * lax.map(spatial_frame, normed)
    placed = sinusoid(jnp.arange(frames, dtype=jnp.int32) + frame_offset[0], model_width, True)
    temporal_in = (residual + placed[:, None, :]).astype(jnp.bfloat16)
    projected = jnp.dot(temporal_in.reshape(frames * frame_tokens, model_width), temporal_qkv, preferred_element_type=jnp.float32).astype(jnp.bfloat16)
    parted = jnp.transpose(projected.reshape(frames, frame_tokens, 3, head_count, HEAD_SIZE), (1, 2, 0, 3, 4))
    mixed = jax.vmap(lambda column: attend(column[0], column[1], column[2]))(parted)
    temporal_mixed = jnp.transpose(mixed, (1, 0, 2)).reshape(frames * frame_tokens, attended)
    temporal_term = jnp.dot(temporal_mixed, temporal_out, preferred_element_type=jnp.float32).reshape(frames, frame_tokens, model_width)
    residual = residual + gate_part * temporal_term
    hidden_out = residual.astype(jnp.bfloat16)
    final_rows = (layer_norm(residual) * final_gain).astype(jnp.bfloat16)
    velocity = jnp.dot(final_rows.reshape(frames * frame_tokens, model_width), out_weight, preferred_element_type=jnp.float32)
    velocity = velocity.reshape(frames, frame_tokens * LCH // 128, 128)
    time_delta = (next_steps - now_steps).astype(jnp.float32) / 1000.0
    update = latents + time_delta[:, None, None] * velocity
    next_latents = jnp.concatenate([fresh_noise[None], update[:-1]], axis=0)
    return (hidden_out, velocity, next_latents)
```

```python
import functools
import math

import jax
import jax.numpy as jnp
from jax import lax
from jax.experimental import pallas as pl
from jax.experimental.pallas import tpu as pltpu
from jax.sharding import PartitionSpec as P

HEAD_SIZE = 72


epsilon = 1e-06


def from_behind(value, axis, steps):
    count = lax.axis_size(axis)
    initial, last = (max(0, -steps), min(count, count - steps))
    return lax.ppermute(value, axis, [(source, source + steps) for source in range(initial, last)])


def layer_norm(values):
    average = jnp.mean(values, axis=-1, keepdims=True)
    centred = values - average
    variance = jnp.mean(centred * centred, axis=-1, keepdims=True)
    return centred * lax.rsqrt(variance + epsilon)


def sinusoid(position, feature_count, first_sine):
    half_width = feature_count // 2
    frequency = jnp.exp(-math.log(10000.0) * jnp.arange(half_width, dtype=jnp.float32) / half_width)
    angles = position.astype(jnp.float32)[:, None] * frequency[None, :]
    if first_sine:
        return jnp.concatenate([jnp.sin(angles), jnp.cos(angles)], axis=-1)
    return jnp.concatenate([jnp.cos(angles), jnp.sin(angles)], axis=-1)


def mix_frames(rows, head_count):
    frame_count = rows.shape[0]
    item_count = rows.shape[1]
    parted = rows.reshape(frame_count, item_count, 3, head_count, HEAD_SIZE)
    attention_scores = jnp.einsum(
        "fnhd,gnhd->nhfg", parted[:, :, 0], parted[:, :, 1], preferred_element_type=jnp.float32
    ) / math.sqrt(HEAD_SIZE)
    row_max = jnp.max(attention_scores, axis=-1, keepdims=True)
    attention_weight = jnp.exp(attention_scores - row_max).astype(jnp.bfloat16)
    denominator = jnp.sum(attention_weight, axis=-1, dtype=jnp.float32)
    weighted_sum = jnp.einsum(
        "nhfg,gnhd->fnhd", attention_weight, parted[:, :, 2], preferred_element_type=jnp.float32
    )
    mixed = weighted_sum / jnp.transpose(denominator, (2, 0, 1))[..., None]
    return mixed.astype(jnp.bfloat16).reshape(frame_count, item_count, head_count * HEAD_SIZE)


def plain_body(
    hidden_in,
    latents,
    fresh_noise,
    level_index,
    time_table,
    frame_offset,
    mod_table,
    time_weight,
    spatial_qkv,
    spatial_out,
    temporal_qkv,
    temporal_out,
    final_gain,
    out_weight,
):
    tokens = hidden_in.shape[1]
    model_width = hidden_in.shape[2]
    attended = spatial_out.shape[0]
    head_count = attended // HEAD_SIZE
    peers = lax.axis_size("frame")
    table_index = jnp.arange(time_table.shape[0], dtype=jnp.int32)
    now_steps = jnp.sum(
        jnp.where(table_index[None, :] == level_index[:, None], time_table[None, :], 0), axis=1
    )
    next_steps = jnp.sum(
        jnp.where(table_index[None, :] == level_index[:, None] - 1, time_table[None, :], 0), axis=1
    )
    activated = jax.nn.silu(sinusoid(now_steps, time_weight.shape[0], False)).astype(jnp.bfloat16)
    modulation = mod_table[None, :] + jnp.dot(
        activated, time_weight, preferred_element_type=jnp.float32
    )
    shift_part = modulation[:, :model_width]
    scale_part = modulation[:, model_width : 2 * model_width]
    gate_part = modulation[:, 2 * model_width :]
    inputs = hidden_in[0].astype(jnp.float32)
    normed = (layer_norm(inputs) * (1.0 + scale_part) + shift_part).astype(jnp.bfloat16)
    projected = jnp.dot(normed, spatial_qkv, preferred_element_type=jnp.float32).astype(
        jnp.bfloat16
    )
    query_rows = projected[:, :attended].reshape(tokens, head_count, HEAD_SIZE)
    key_value = projected[:, attended:]
    block_rows = lax.all_gather(key_value, "band", axis=0, tiled=True)
    row_max = jnp.full((head_count, tokens), -1e30, jnp.float32)
    row_count = block_rows.shape[0]
    key_matrix_rows = block_rows[:, :attended].reshape(row_count, head_count, HEAD_SIZE)
    value_matrix_rows = block_rows[:, attended:].reshape(row_count, head_count, HEAD_SIZE)
    attention_scores = jnp.einsum(
        "ubg,wbg->buw", query_rows, key_matrix_rows, preferred_element_type=jnp.float32
    ) / math.sqrt(HEAD_SIZE)
    new_max = jnp.maximum(row_max, jnp.max(attention_scores, axis=-1))
    attention_weight = jnp.exp(attention_scores - new_max[:, :, None]).astype(jnp.bfloat16)
    denominator = jnp.sum(attention_weight, axis=-1, dtype=jnp.float32)
    weighted_sum = jnp.einsum(
        "leq,qlr->ler", attention_weight, value_matrix_rows, preferred_element_type=jnp.float32
    )
    row_max, denominator, weighted_sum = (new_max, denominator, weighted_sum)
    spatial_mixed = (
        jnp.transpose(weighted_sum / denominator[:, :, None], (1, 0, 2))
        .reshape(tokens, attended)
        .astype(jnp.bfloat16)
    )
    residual = inputs + gate_part * jnp.dot(
        spatial_mixed, spatial_out, preferred_element_type=jnp.float32
    )
    position = lax.axis_index("frame") + frame_offset
    placed = sinusoid(position, model_width, True)
    temporal_in = (residual + placed).astype(jnp.bfloat16)
    spread_rows = temporal_in.reshape(1, peers, tokens // peers, model_width)
    gathered = lax.all_to_all(spread_rows, "frame", split_axis=1, concat_axis=0, tiled=True)
    frame_count = gathered.shape[0]
    item_count = gathered.shape[2]
    rows = jnp.dot(
        gathered.reshape(frame_count * item_count, model_width),
        temporal_qkv,
        preferred_element_type=jnp.float32,
    ).astype(jnp.bfloat16)
    mixed = mix_frames(rows.reshape(frame_count, item_count, 3 * attended), head_count)
    mixed_rows = mixed.reshape(frame_count, 1, item_count, attended)
    mixed_pairs = mixed_rows.reshape(mixed_rows.shape[0], 1, mixed_rows.shape[2] // 2, 2 * attended)
    returned = lax.all_to_all(mixed_pairs, "frame", split_axis=0, concat_axis=1, tiled=True)
    temporal_mixed = returned.reshape(tokens, attended)
    residual = residual + gate_part * jnp.dot(
        temporal_mixed, temporal_out, preferred_element_type=jnp.float32
    )
    hidden_out = residual.astype(jnp.bfloat16)[None]
    final_rows = (layer_norm(residual) * final_gain).astype(jnp.bfloat16)
    velocity = jnp.dot(final_rows, out_weight, preferred_element_type=jnp.float32).reshape(
        1, latents.shape[1], 128
    )
    time_delta = (next_steps - now_steps).astype(jnp.float32) / 1000.0
    update = latents + time_delta[:, None, None] * velocity
    shifted = from_behind(update.astype(jnp.bfloat16), "frame", 1).astype(update.dtype)
    next_latents = jnp.where(lax.axis_index("frame") == 0, fresh_noise[None], shifted)
    return (hidden_out, velocity, next_latents)


MESH = pl.DeviceIdType.MESH
ROWS = 256
PAIR = 2
GROUP = 16
LANES = 128


def block_kernel(
    peers,
    head_count,
    hidden,
    mod,
    placed,
    gain,
    wide_weight,
    time_delta,
    latents,
    noise,
    spatial_qkv_hbm,
    spatial_out_hbm,
    temporal_qkv_hbm,
    temporal_out_hbm,
    hidden_out,
    velocity_out,
    next_out,
    spatial_qkv,
    spatial_out,
    temporal_qkv,
    temporal_out,
    normed,
    projected,
    remote_kv,
    query,
    key,
    value,
    head_out,
    mixed,
    residual,
    outgoing,
    gathered,
    temporal,
    answer,
    returned,
    update_sent,
    update_received,
    weight_sem,
    kv_send,
    kv_recv,
    fwd_send,
    fwd_recv,
    ret_send,
    ret_recv,
    next_send,
    next_recv,
):
    f32, bf16 = jnp.float32, jnp.bfloat16
    tokens, width = hidden.shape
    attended = head_count * HEAD_SIZE
    item = tokens // peers
    me = lax.axis_index("frame")
    mate = 1 - lax.axis_index("band")
    pairs = peers // PAIR
    my_pair = me // PAIR
    chunk = PAIR * item
    first_kv = attended // LANES * LANES
    kv_shift = attended - first_kv
    query_factor = math.log2(math.e) / math.sqrt(HEAD_SIZE)

    loads = [
        pltpu.make_async_copy(source, target, weight_sem.at[index])
        for index, (source, target) in enumerate(
            (
                (spatial_qkv_hbm, spatial_qkv),
                (spatial_out_hbm, spatial_out),
                (temporal_qkv_hbm, temporal_qkv),
                (temporal_out_hbm, temporal_out),
            )
        )
    ]
    for load in loads:
        load.start()

    barrier = pltpu.get_barrier_semaphore()
    pl.semaphore_signal(barrier, inc=1, device_id={"band": mate}, device_id_type=MESH)
    for step in range(1, peers):
        pl.semaphore_signal(
            barrier, inc=1, device_id={"frame": lax.rem(me + step, peers)}, device_id_type=MESH
        )

    column = lax.broadcasted_iota(jnp.int32, (1, 3 * attended), 1)
    column_factor = jnp.where(column < attended, query_factor, 1.0).astype(f32)
    gate = mod[:, 2 * width :]

    def norm_step(index, carry):
        rows = pl.ds(pl.multiple_of(index * 64, 64), 64)
        lines = layer_norm(hidden[rows, :].astype(f32))
        normed[rows, :] = (lines * (1.0 + mod[:, width : 2 * width]) + mod[:, :width]).astype(bf16)
        return carry

    lax.fori_loop(0, tokens // 64, norm_step, 0)
    query[...] = jnp.zeros_like(query)
    key[...] = jnp.zeros_like(key)
    value[...] = jnp.ones_like(value)
    pl.semaphore_wait(barrier, peers)
    loads[0].wait()

    def kv_copy(index):
        rows = pl.ds(pl.multiple_of(index * ROWS, ROWS), ROWS)
        return pltpu.make_async_remote_copy(
            src_ref=projected.at[rows, pl.ds(first_kv, 3 * attended - first_kv)],
            dst_ref=remote_kv.at[rows, :],
            send_sem=kv_send.at[index],
            recv_sem=kv_recv.at[index],
            device_id={"band": mate},
            device_id_type=MESH,
        )

    def project_step(index, carry):
        rows = pl.ds(pl.multiple_of(index * ROWS, ROWS), ROWS)
        product = jnp.dot(normed[rows, :], spatial_qkv[...], preferred_element_type=f32)
        projected[rows, :] = (product * column_factor).astype(bf16)
        kv_copy(index).start()
        return carry

    lax.fori_loop(0, tokens // ROWS, project_step, 0)

    def split_own(index, carry):
        rows = pl.ds(pl.multiple_of(index * ROWS, ROWS), ROWS)
        for head in range(head_count):
            low = head * HEAD_SIZE
            query[head, rows, :HEAD_SIZE] = projected[rows, low : low + HEAD_SIZE]
            low += attended
            key[head, rows, :HEAD_SIZE] = projected[rows, low : low + HEAD_SIZE]
            low += attended
            value[head, rows, :HEAD_SIZE] = projected[rows, low : low + HEAD_SIZE]
        return carry

    lax.fori_loop(0, tokens // ROWS, split_own, 0)

    def split_remote(index, carry):
        kv_copy(index).wait_recv()
        rows = pl.ds(pl.multiple_of(index * ROWS, ROWS), ROWS)
        there = pl.ds(pl.multiple_of(tokens + index * ROWS, ROWS), ROWS)
        for head in range(head_count):
            low = head * HEAD_SIZE + kv_shift
            key[head, there, :HEAD_SIZE] = remote_kv[rows, low : low + HEAD_SIZE]
            low += attended
            value[head, there, :HEAD_SIZE] = remote_kv[rows, low : low + HEAD_SIZE]
        return carry

    lax.fori_loop(0, tokens // ROWS, split_remote, 0)
    loads[1].wait()

    def forward_copy(source, target):
        return pltpu.make_async_remote_copy(
            src_ref=outgoing.at[target],
            dst_ref=gathered.at[source],
            send_sem=fwd_send.at[target],
            recv_sem=fwd_recv.at[source],
            device_id={"frame": target},
            device_id_type=MESH,
        )

    def query_step(index, carry):
        pair = lax.rem(my_pair + 1 + index, pairs)
        rows = pl.ds(pl.multiple_of(pair * chunk, chunk), chunk)

        def head_step(half, inner):
            for part in range(2):
                head = half * 2 + part
                scores = lax.dot_general(
                    query[head, rows, :],
                    key[head],
                    (((1,), (1,)), ((), ())),
                    preferred_element_type=f32,
                )
                top = jnp.max(scores, axis=-1, keepdims=True)
                weight = jnp.exp2(scores - top).astype(bf16)
                total = jnp.dot(weight, value[head], preferred_element_type=f32)
                head_out[head] = (total / total[:, HEAD_SIZE : HEAD_SIZE + 1]).astype(bf16)
            return inner

        lax.fori_loop(0, head_count // 2, head_step, 0)
        for head in range(head_count):
            mixed[:, head * HEAD_SIZE : (head + 1) * HEAD_SIZE] = head_out[head, :, :HEAD_SIZE]
        product = jnp.dot(mixed[...], spatial_out[...], preferred_element_type=f32)
        lines = hidden[rows, :].astype(f32) + gate * product
        residual[rows, :] = lines
        sent = (lines + placed[...]).astype(bf16)
        for part in range(PAIR):
            target = pair * PAIR + part
            outgoing[target] = sent[part * item : (part + 1) * item]

            @pl.when(target != me)
            def _():
                forward_copy(me, target).start()

            @pl.when(target == me)
            def _():
                gathered[target] = sent[part * item : (part + 1) * item]

        return carry

    lax.fori_loop(0, pairs, query_step, 0)
    loads[2].wait()

    def temporal_step(index, carry):
        pair = lax.rem(my_pair + 2 * pairs - 1 - index, pairs)
        for part in range(PAIR):
            source = pair * PAIR + part

            @pl.when(source != me)
            def _():
                forward_copy(source, source).wait_recv()

        lines = gathered[pl.ds(pair * PAIR, PAIR)].reshape(chunk, width)
        product = jnp.dot(lines, temporal_qkv[...], preferred_element_type=f32)
        temporal[pl.ds(pair * PAIR, PAIR)] = (
            (product * column_factor).astype(bf16).reshape(PAIR, item, 3 * attended)
        )
        return carry

    lax.fori_loop(0, pairs, temporal_step, 0)

    count = peers * GROUP
    row_item = lax.rem(lax.broadcasted_iota(jnp.int32, (count, count), 0), GROUP)
    column_item = lax.rem(lax.broadcasted_iota(jnp.int32, (count, count), 1), GROUP)
    same_item = row_item == column_item
    lowest = float(jnp.finfo(f32).min)
    half_item = item // 2

    def return_copy(source, target, half):
        rows = pl.ds(pl.multiple_of(half * half_item, half_item), half_item)
        return pltpu.make_async_remote_copy(
            src_ref=answer.at[target, rows, :],
            dst_ref=returned.at[source, rows, :],
            send_sem=ret_send.at[target, half],
            recv_sem=ret_recv.at[source, half],
            device_id={"frame": target},
            device_id_type=MESH,
        )

    def half_step(half, carry):
        def group_step(group, inner):
            start = pl.multiple_of(half * half_item + group * GROUP, GROUP)
            rows = pl.ds(start, GROUP)
            lines = temporal[:, rows, :].reshape(count, 3 * attended)
            for head in range(head_count):
                low = head * HEAD_SIZE
                scores = lax.dot_general(
                    lines[:, low : low + HEAD_SIZE],
                    lines[:, attended + low : attended + low + HEAD_SIZE],
                    (((1,), (1,)), ((), ())),
                    preferred_element_type=f32,
                )
                scores = jnp.where(same_item, scores, lowest)
                top = jnp.max(scores, axis=-1, keepdims=True)
                weight = jnp.exp2(scores - top).astype(bf16)
                denominator = jnp.sum(weight.astype(f32), axis=-1, keepdims=True)
                total = jnp.dot(
                    weight,
                    lines[:, 2 * attended + low : 2 * attended + low + HEAD_SIZE],
                    preferred_element_type=f32,
                )
                answer[:, rows, low : low + HEAD_SIZE] = (
                    (total / denominator).astype(bf16).reshape(peers, GROUP, HEAD_SIZE)
                )
            return inner

        lax.fori_loop(0, half_item // GROUP, group_step, 0)

        def send_step(step, inner):
            return_copy(me, lax.rem(me + step, peers), half).start()
            return inner

        lax.fori_loop(1, peers, send_step, 0)
        return carry

    lax.fori_loop(0, 2, half_step, 0)
    returned[me] = answer[me]
    loads[3].wait()

    velocity_rows = chunk * (width // width) // 8
    lane = lax.broadcasted_iota(jnp.int32, (chunk, LANES), 1)
    line = lax.broadcasted_iota(jnp.int32, (chunk, LANES), 0)
    keep = lane // (LANES // 8) == lax.rem(line, 8)

    def final_step(index, carry):
        pair = lax.rem(my_pair + index, pairs)
        for part in range(PAIR):
            source = pair * PAIR + part

            @pl.when(source != me)
            def _():
                return_copy(source, source, 0).wait_recv()
                return_copy(source, source, 1).wait_recv()

        rows = pl.ds(pl.multiple_of(pair * chunk, chunk), chunk)
        lines = returned[pl.ds(pair * PAIR, PAIR)].reshape(chunk, attended)
        product = jnp.dot(lines, temporal_out[...], preferred_element_type=f32)
        block = residual[rows, :] + gate * product
        hidden_out[rows, :] = block.astype(bf16)
        final_rows = (layer_norm(block) * gain[...]).astype(bf16)
        wide = jnp.dot(final_rows, wide_weight[...], preferred_element_type=f32)
        packed = jnp.sum(jnp.where(keep, wide, 0.0).reshape(velocity_rows, 8, LANES), axis=1)
        velocity_out[pl.ds(pl.multiple_of(pair * velocity_rows, velocity_rows), velocity_rows), :] = (
            packed
        )
        return carry

    lax.fori_loop(0, pairs, final_step, 0)
    update_sent[...] = (latents[...] + time_delta[0, 0] * velocity_out[...]).astype(bf16)
    next_copy = pltpu.make_async_remote_copy(
        src_ref=update_sent,
        dst_ref=update_received,
        send_sem=next_send,
        recv_sem=next_recv,
        device_id={"frame": lax.rem(me + 1, peers)},
        device_id_type=MESH,
    )
    next_copy.start()

    def drain(index, carry):
        kv_copy(index).wait_send()
        return carry

    lax.fori_loop(0, tokens // ROWS, drain, 0)

    def drain_peer(step, carry):
        target = lax.rem(me + step, peers)
        forward_copy(me, target).wait_send()
        return_copy(me, target, 0).wait_send()
        return_copy(me, target, 1).wait_send()
        return carry

    lax.fori_loop(1, peers, drain_peer, 0)
    next_copy.wait()

    @pl.when(me == 0)
    def _():
        next_out[...] = noise[...]

    @pl.when(me != 0)
    def _():
        next_out[...] = update_received[...].astype(f32)


def body(
    hidden_in,
    latents,
    fresh_noise,
    level_index,
    time_table,
    frame_offset,
    mod_table,
    time_weight,
    spatial_qkv,
    spatial_out,
    temporal_qkv,
    temporal_out,
    final_gain,
    out_weight,
):
    tokens, width = hidden_in.shape[1:]
    attended = spatial_out.shape[0]
    head_count = attended // HEAD_SIZE
    peers = lax.axis_size("frame")
    item = tokens // peers
    fits = (
        peers % PAIR == 0
        and tokens % ROWS == 0
        and item % (2 * GROUP) == 0
        and head_count % 2 == 0
        and lax.axis_size("band") == 2
        and peers * GROUP <= LANES
        and out_weight.shape[1] * 8 == LANES
    )
    if not fits:
        return plain_body(
            hidden_in,
            latents,
            fresh_noise,
            level_index,
            time_table,
            frame_offset,
            mod_table,
            time_weight,
            spatial_qkv,
            spatial_out,
            temporal_qkv,
            temporal_out,
            final_gain,
            out_weight,
        )
    table_index = jnp.arange(time_table.shape[0], dtype=jnp.int32)
    now_steps = jnp.sum(
        jnp.where(table_index[None, :] == level_index[:, None], time_table[None, :], 0), axis=1
    )
    next_steps = jnp.sum(
        jnp.where(table_index[None, :] == level_index[:, None] - 1, time_table[None, :], 0), axis=1
    )
    activated = jax.nn.silu(sinusoid(now_steps, time_weight.shape[0], False)).astype(jnp.bfloat16)
    modulation = mod_table[None, :] + jnp.dot(
        activated, time_weight, preferred_element_type=jnp.float32
    )
    placed = sinusoid(lax.axis_index("frame") + frame_offset, width, True)
    time_delta = ((next_steps - now_steps).astype(jnp.float32) / 1000.0).reshape(1, 1)
    wide_weight = jnp.tile(out_weight, (1, 8))
    bf16, f32 = jnp.bfloat16, jnp.float32
    vmem = pl.BlockSpec(memory_space=pltpu.VMEM)
    anywhere = pl.BlockSpec(memory_space=pl.ANY)
    steps = tokens // ROWS
    chunk = PAIR * item
    dma = pltpu.SemaphoreType.DMA
    latent_rows = latents.shape[1]
    hidden_out, velocity, next_latents = pl.pallas_call(
        functools.partial(block_kernel, peers, head_count),
        out_shape=(
            jax.ShapeDtypeStruct((tokens, width), bf16),
            jax.ShapeDtypeStruct((latent_rows, LANES), f32),
            jax.ShapeDtypeStruct((latent_rows, LANES), f32),
        ),
        in_specs=[vmem] * 5
        + [pl.BlockSpec(memory_space=pltpu.SMEM)]
        + [vmem] * 2
        + [anywhere] * 4,
        out_specs=(vmem, vmem, vmem),
        scratch_shapes=[
            pltpu.VMEM(spatial_qkv.shape, bf16),
            pltpu.VMEM(spatial_out.shape, bf16),
            pltpu.VMEM(temporal_qkv.shape, bf16),
            pltpu.VMEM(temporal_out.shape, bf16),
            pltpu.VMEM((tokens, width), bf16),
            pltpu.VMEM((tokens, 3 * attended), bf16),
            pltpu.VMEM((tokens, 3 * attended - attended // LANES * LANES), bf16),
            pltpu.VMEM((head_count, tokens, LANES), bf16),
            pltpu.VMEM((head_count, 2 * tokens, LANES), bf16),
            pltpu.VMEM((head_count, 2 * tokens, LANES), bf16),
            pltpu.VMEM((head_count, chunk, LANES), bf16),
            pltpu.VMEM((chunk, attended), bf16),
            pltpu.VMEM((tokens, width), f32),
            pltpu.VMEM((peers, item, width), bf16),
            pltpu.VMEM((peers, item, width), bf16),
            pltpu.VMEM((peers, item, 3 * attended), bf16),
            pltpu.VMEM((peers, item, attended), bf16),
            pltpu.VMEM((peers, item, attended), bf16),
            pltpu.VMEM((latent_rows, LANES), bf16),
            pltpu.VMEM((latent_rows, LANES), bf16),
            dma((4,)),
            dma((steps,)),
            dma((steps,)),
            dma((peers,)),
            dma((peers,)),
            dma((peers, 2)),
            dma((peers, 2)),
            dma,
            dma,
        ],
        compiler_params=pltpu.CompilerParams(
            collective_id=0, has_side_effects=True, vmem_limit_bytes=63 * 1024 * 1024
        ),
        name="block",
    )(
        hidden_in[0],
        modulation,
        placed,
        final_gain[None, :],
        wide_weight,
        time_delta,
        latents[0],
        fresh_noise,
        spatial_qkv,
        spatial_out,
        temporal_qkv,
        temporal_out,
    )
    return (hidden_out[None], velocity[None], next_latents[None])


def solution(mesh):
    placed = (
        P(("groups", "frame"), "band", None),
        P(("groups", "frame"), "band", None),
        P(("groups", "band"), None),
        P(("groups", "frame")),
        P(),
        P("groups"),
        P(),
        P(),
        P(),
        P(),
        P(),
        P(),
        P(),
        P(),
    )
    return jax.shard_map(
        body,
        mesh=mesh,
        in_specs=placed,
        out_specs=(
            P(("groups", "frame"), "band", None),
            P(("groups", "frame"), "band", None),
            P(("groups", "frame"), "band", None),
        ),
        check_vma=False,
    )
```

```python
import functools
import math

import jax
import jax.numpy as jnp
import numpy as np
from jax import lax
from jax.experimental import pallas as pl
from jax.experimental.pallas import tpu as pltpu
from jax.sharding import PartitionSpec as P

HEAD_SIZE = 72


epsilon = 1e-06


def from_behind(value, axis, steps):
    count = lax.axis_size(axis)
    initial, last = (max(0, -steps), min(count, count - steps))
    return lax.ppermute(value, axis, [(source, source + steps) for source in range(initial, last)])


def layer_norm(values):
    average = jnp.mean(values, axis=-1, keepdims=True)
    centred = values - average
    variance = jnp.mean(centred * centred, axis=-1, keepdims=True)
    return centred * lax.rsqrt(variance + epsilon)


def sinusoid(position, feature_count, first_sine):
    half_width = feature_count // 2
    frequency = jnp.exp(-math.log(10000.0) * jnp.arange(half_width, dtype=jnp.float32) / half_width)
    angles = position.astype(jnp.float32)[:, None] * frequency[None, :]
    if first_sine:
        return jnp.concatenate([jnp.sin(angles), jnp.cos(angles)], axis=-1)
    return jnp.concatenate([jnp.cos(angles), jnp.sin(angles)], axis=-1)


def mix_frames(rows, head_count):
    frame_count = rows.shape[0]
    item_count = rows.shape[1]
    parted = rows.reshape(frame_count, item_count, 3, head_count, HEAD_SIZE)
    attention_scores = jnp.einsum(
        "fnhd,gnhd->nhfg", parted[:, :, 0], parted[:, :, 1], preferred_element_type=jnp.float32
    ) / math.sqrt(HEAD_SIZE)
    row_max = jnp.max(attention_scores, axis=-1, keepdims=True)
    attention_weight = jnp.exp(attention_scores - row_max).astype(jnp.bfloat16)
    denominator = jnp.sum(attention_weight, axis=-1, dtype=jnp.float32)
    weighted_sum = jnp.einsum(
        "nhfg,gnhd->fnhd", attention_weight, parted[:, :, 2], preferred_element_type=jnp.float32
    )
    mixed = weighted_sum / jnp.transpose(denominator, (2, 0, 1))[..., None]
    return mixed.astype(jnp.bfloat16).reshape(frame_count, item_count, head_count * HEAD_SIZE)


def plain_body(
    hidden_in,
    latents,
    fresh_noise,
    level_index,
    time_table,
    frame_offset,
    mod_table,
    time_weight,
    spatial_qkv,
    spatial_out,
    temporal_qkv,
    temporal_out,
    final_gain,
    out_weight,
):
    tokens = hidden_in.shape[1]
    model_width = hidden_in.shape[2]
    attended = spatial_out.shape[0]
    head_count = attended // HEAD_SIZE
    peers = lax.axis_size("frame")
    table_index = jnp.arange(time_table.shape[0], dtype=jnp.int32)
    now_steps = jnp.sum(
        jnp.where(table_index[None, :] == level_index[:, None], time_table[None, :], 0), axis=1
    )
    next_steps = jnp.sum(
        jnp.where(table_index[None, :] == level_index[:, None] - 1, time_table[None, :], 0), axis=1
    )
    activated = jax.nn.silu(sinusoid(now_steps, time_weight.shape[0], False)).astype(jnp.bfloat16)
    modulation = mod_table[None, :] + jnp.dot(
        activated, time_weight, preferred_element_type=jnp.float32
    )
    shift_part = modulation[:, :model_width]
    scale_part = modulation[:, model_width : 2 * model_width]
    gate_part = modulation[:, 2 * model_width :]
    inputs = hidden_in[0].astype(jnp.float32)
    normed = (layer_norm(inputs) * (1.0 + scale_part) + shift_part).astype(jnp.bfloat16)
    projected = jnp.dot(normed, spatial_qkv, preferred_element_type=jnp.float32).astype(
        jnp.bfloat16
    )
    query_rows = projected[:, :attended].reshape(tokens, head_count, HEAD_SIZE)
    key_value = projected[:, attended:]
    block_rows = lax.all_gather(key_value, "band", axis=0, tiled=True)
    row_max = jnp.full((head_count, tokens), -1e30, jnp.float32)
    row_count = block_rows.shape[0]
    key_matrix_rows = block_rows[:, :attended].reshape(row_count, head_count, HEAD_SIZE)
    value_matrix_rows = block_rows[:, attended:].reshape(row_count, head_count, HEAD_SIZE)
    attention_scores = jnp.einsum(
        "ubg,wbg->buw", query_rows, key_matrix_rows, preferred_element_type=jnp.float32
    ) / math.sqrt(HEAD_SIZE)
    new_max = jnp.maximum(row_max, jnp.max(attention_scores, axis=-1))
    attention_weight = jnp.exp(attention_scores - new_max[:, :, None]).astype(jnp.bfloat16)
    denominator = jnp.sum(attention_weight, axis=-1, dtype=jnp.float32)
    weighted_sum = jnp.einsum(
        "leq,qlr->ler", attention_weight, value_matrix_rows, preferred_element_type=jnp.float32
    )
    row_max, denominator, weighted_sum = (new_max, denominator, weighted_sum)
    spatial_mixed = (
        jnp.transpose(weighted_sum / denominator[:, :, None], (1, 0, 2))
        .reshape(tokens, attended)
        .astype(jnp.bfloat16)
    )
    residual = inputs + gate_part * jnp.dot(
        spatial_mixed, spatial_out, preferred_element_type=jnp.float32
    )
    position = lax.axis_index("frame") + frame_offset
    placed = sinusoid(position, model_width, True)
    temporal_in = (residual + placed).astype(jnp.bfloat16)
    spread_rows = temporal_in.reshape(1, peers, tokens // peers, model_width)
    gathered = lax.all_to_all(spread_rows, "frame", split_axis=1, concat_axis=0, tiled=True)
    frame_count = gathered.shape[0]
    item_count = gathered.shape[2]
    rows = jnp.dot(
        gathered.reshape(frame_count * item_count, model_width),
        temporal_qkv,
        preferred_element_type=jnp.float32,
    ).astype(jnp.bfloat16)
    mixed = mix_frames(rows.reshape(frame_count, item_count, 3 * attended), head_count)
    mixed_rows = mixed.reshape(frame_count, 1, item_count, attended)
    mixed_pairs = mixed_rows.reshape(mixed_rows.shape[0], 1, mixed_rows.shape[2] // 2, 2 * attended)
    returned = lax.all_to_all(mixed_pairs, "frame", split_axis=0, concat_axis=1, tiled=True)
    temporal_mixed = returned.reshape(tokens, attended)
    residual = residual + gate_part * jnp.dot(
        temporal_mixed, temporal_out, preferred_element_type=jnp.float32
    )
    hidden_out = residual.astype(jnp.bfloat16)[None]
    final_rows = (layer_norm(residual) * final_gain).astype(jnp.bfloat16)
    velocity = jnp.dot(final_rows, out_weight, preferred_element_type=jnp.float32).reshape(
        1, latents.shape[1], 128
    )
    time_delta = (next_steps - now_steps).astype(jnp.float32) / 1000.0
    update = latents + time_delta[:, None, None] * velocity
    shifted = from_behind(update.astype(jnp.bfloat16), "frame", 1).astype(update.dtype)
    next_latents = jnp.where(lax.axis_index("frame") == 0, fresh_noise[None], shifted)
    return (hidden_out, velocity, next_latents)


MESH = pl.DeviceIdType.MESH
ROWS = 256
PAIR = 2
GROUP = 16
LANES = 128


def times_turned(rows, turned):
    return lax.dot_general(
        rows, turned, (((1,), (1,)), ((), ())), preferred_element_type=jnp.float32
    )


def block_kernel(
    peers,
    head_count,
    hidden,
    level_index,
    time_table,
    frame_offset,
    time_frequency,
    place_frequency,
    mod_table,
    time_weight,
    final_gain,
    out_weight,
    latents,
    noise,
    spatial_qkv_hbm,
    spatial_out_hbm,
    temporal_qkv_hbm,
    temporal_out_hbm,
    hidden_out,
    velocity_out,
    next_out,
    spatial_qkv,
    spatial_out,
    temporal_qkv,
    temporal_out,
    normed,
    projected,
    remote_kv,
    query,
    key,
    value,
    head_out,
    mixed,
    mod,
    placed,
    gain,
    wide_weight,
    residual,
    outgoing,
    gathered,
    temporal,
    answer,
    returned,
    update_sent,
    update_received,
    weight_sem,
    kv_send,
    kv_recv,
    fwd_send,
    fwd_recv,
    ret_send,
    ret_recv,
    next_send,
    next_recv,
):
    f32, bf16 = jnp.float32, jnp.bfloat16
    tokens, width = hidden.shape
    attended = head_count * HEAD_SIZE
    item = tokens // peers
    me = lax.axis_index("frame")
    mate = 1 - lax.axis_index("band")
    pairs = peers // PAIR
    my_pair = me // PAIR
    chunk = PAIR * item
    first_kv = attended // LANES * LANES
    kv_shift = attended - first_kv
    query_factor = math.log2(math.e) / math.sqrt(HEAD_SIZE)

    loads = [
        pltpu.make_async_copy(source, target, weight_sem.at[index])
        for index, (source, target) in enumerate(
            (
                (spatial_qkv_hbm, spatial_qkv),
                (spatial_out_hbm, spatial_out),
                (temporal_qkv_hbm, temporal_qkv),
                (temporal_out_hbm, temporal_out),
            )
        )
    ]
    for load in loads:
        load.start()

    barrier = pltpu.get_barrier_semaphore()
    pl.semaphore_signal(barrier, inc=1, device_id={"band": mate}, device_id_type=MESH)
    for step in range(1, peers):
        pl.semaphore_signal(
            barrier, inc=1, device_id={"frame": lax.rem(me + step, peers)}, device_id_type=MESH
        )

    table = time_table[...].reshape(1, time_table.shape[0]).astype(f32)
    entry = lax.broadcasted_iota(jnp.int32, table.shape, 1)
    level = level_index[0]
    now_step = jnp.sum(jnp.where(entry == level, table, 0.0), axis=1, keepdims=True)
    next_step = jnp.sum(jnp.where(entry == level - 1, table, 0.0), axis=1, keepdims=True)
    time_delta = (next_step - now_step) / 1000.0
    angles = now_step * time_frequency[...]
    activated = jax.nn.silu(jnp.concatenate([jnp.cos(angles), jnp.sin(angles)], axis=-1))
    mod[...] = mod_table[...].reshape(1, 3 * width) + jnp.dot(
        activated.astype(bf16), time_weight[...], preferred_element_type=f32
    )
    places = (me + frame_offset[0]).astype(f32) * place_frequency[...]
    placed[...] = jnp.concatenate([jnp.sin(places), jnp.cos(places)], axis=-1)
    gain[...] = final_gain[...].reshape(1, width)
    for copy in range(8):
        wide_weight[copy * (LANES // 8) : (copy + 1) * (LANES // 8), :] = out_weight[...]
    column = lax.broadcasted_iota(jnp.int32, (1, 3 * attended), 1)
    column_factor = jnp.where(column < attended, query_factor, 1.0).astype(f32)
    gate = mod[:, 2 * width :]

    def norm_step(index, carry):
        rows = pl.ds(pl.multiple_of(index * 64, 64), 64)
        lines = layer_norm(hidden[rows, :].astype(f32))
        normed[rows, :] = (lines * (1.0 + mod[:, width : 2 * width]) + mod[:, :width]).astype(bf16)
        return carry

    lax.fori_loop(0, tokens // 64, norm_step, 0)
    query[...] = jnp.zeros_like(query)
    key[...] = jnp.zeros_like(key)
    value[...] = jnp.ones_like(value)
    pl.semaphore_wait(barrier, peers)
    loads[0].wait()

    def kv_copy(index):
        rows = pl.ds(pl.multiple_of(index * ROWS, ROWS), ROWS)
        return pltpu.make_async_remote_copy(
            src_ref=projected.at[rows, pl.ds(first_kv, 3 * attended - first_kv)],
            dst_ref=remote_kv.at[rows, :],
            send_sem=kv_send.at[index],
            recv_sem=kv_recv.at[index],
            device_id={"band": mate},
            device_id_type=MESH,
        )

    def project_step(index, carry):
        rows = pl.ds(pl.multiple_of(index * ROWS, ROWS), ROWS)
        product = times_turned(normed[rows, :], spatial_qkv[...])
        projected[rows, :] = (product * column_factor).astype(bf16)
        kv_copy(index).start()
        return carry

    lax.fori_loop(0, tokens // ROWS, project_step, 0)

    def split_own(index, carry):
        rows = pl.ds(pl.multiple_of(index * ROWS, ROWS), ROWS)
        for head in range(head_count):
            low = head * HEAD_SIZE
            query[head, rows, :HEAD_SIZE] = projected[rows, low : low + HEAD_SIZE]
            low += attended
            key[head, rows, :HEAD_SIZE] = projected[rows, low : low + HEAD_SIZE]
            low += attended
            value[head, rows, :HEAD_SIZE] = projected[rows, low : low + HEAD_SIZE]
        return carry

    lax.fori_loop(0, tokens // ROWS, split_own, 0)

    def split_remote(index, carry):
        kv_copy(index).wait_recv()
        rows = pl.ds(pl.multiple_of(index * ROWS, ROWS), ROWS)
        there = pl.ds(pl.multiple_of(tokens + index * ROWS, ROWS), ROWS)
        for head in range(head_count):
            low = head * HEAD_SIZE + kv_shift
            key[head, there, :HEAD_SIZE] = remote_kv[rows, low : low + HEAD_SIZE]
            low += attended
            value[head, there, :HEAD_SIZE] = remote_kv[rows, low : low + HEAD_SIZE]
        return carry

    lax.fori_loop(0, tokens // ROWS, split_remote, 0)
    loads[1].wait()

    def forward_copy(source, target):
        return pltpu.make_async_remote_copy(
            src_ref=outgoing.at[target],
            dst_ref=gathered.at[source],
            send_sem=fwd_send.at[target],
            recv_sem=fwd_recv.at[source],
            device_id={"frame": target},
            device_id_type=MESH,
        )

    def query_step(index, carry):
        pair = lax.rem(my_pair + 1 + index, pairs)
        rows = pl.ds(pl.multiple_of(pair * chunk, chunk), chunk)

        def head_step(half, inner):
            for part in range(2):
                head = half * 2 + part
                scores = lax.dot_general(
                    query[head, rows, :],
                    key[head],
                    (((1,), (1,)), ((), ())),
                    preferred_element_type=f32,
                )
                top = jnp.max(scores, axis=-1, keepdims=True)
                weight = jnp.exp2(scores - top).astype(bf16)
                total = jnp.dot(weight, value[head], preferred_element_type=f32)
                head_out[head] = (total / total[:, HEAD_SIZE : HEAD_SIZE + 1]).astype(bf16)
            return inner

        lax.fori_loop(0, head_count // 2, head_step, 0)
        for head in range(head_count):
            mixed[:, head * HEAD_SIZE : (head + 1) * HEAD_SIZE] = head_out[head, :, :HEAD_SIZE]
        product = jnp.dot(mixed[...], spatial_out[...], preferred_element_type=f32)
        lines = hidden[rows, :].astype(f32) + gate * product
        residual[rows, :] = lines
        sent = (lines + placed[...]).astype(bf16)
        for part in range(PAIR):
            target = pair * PAIR + part
            outgoing[target] = sent[part * item : (part + 1) * item]

            @pl.when(target != me)
            def _():
                forward_copy(me, target).start()

            @pl.when(target == me)
            def _():
                gathered[target] = sent[part * item : (part + 1) * item]

        return carry

    lax.fori_loop(0, pairs, query_step, 0)
    loads[2].wait()

    def temporal_step(index, carry):
        pair = lax.rem(my_pair + 2 * pairs - 1 - index, pairs)
        for part in range(PAIR):
            source = pair * PAIR + part

            @pl.when(source != me)
            def _():
                forward_copy(source, source).wait_recv()

        lines = gathered[pl.ds(pair * PAIR, PAIR)].reshape(chunk, width)
        product = times_turned(lines, temporal_qkv[...])
        temporal[pl.ds(pair * PAIR, PAIR)] = (
            (product * column_factor).astype(bf16).reshape(PAIR, item, 3 * attended)
        )
        return carry

    lax.fori_loop(0, pairs, temporal_step, 0)

    count = peers * GROUP
    row_item = lax.rem(lax.broadcasted_iota(jnp.int32, (count, count), 0), GROUP)
    column_item = lax.rem(lax.broadcasted_iota(jnp.int32, (count, count), 1), GROUP)
    same_item = row_item == column_item
    lowest = float(jnp.finfo(f32).min)
    half_item = item // 2

    def return_copy(source, target, half):
        rows = pl.ds(pl.multiple_of(half * half_item, half_item), half_item)
        return pltpu.make_async_remote_copy(
            src_ref=answer.at[target, rows, :],
            dst_ref=returned.at[source, rows, :],
            send_sem=ret_send.at[target, half],
            recv_sem=ret_recv.at[source, half],
            device_id={"frame": target},
            device_id_type=MESH,
        )

    def half_step(half, carry):
        def group_step(group, inner):
            start = pl.multiple_of(half * half_item + group * GROUP, GROUP)
            rows = pl.ds(start, GROUP)
            lines = temporal[:, rows, :].reshape(count, 3 * attended)
            for head in range(head_count):
                low = head * HEAD_SIZE
                scores = lax.dot_general(
                    lines[:, low : low + HEAD_SIZE],
                    lines[:, attended + low : attended + low + HEAD_SIZE],
                    (((1,), (1,)), ((), ())),
                    preferred_element_type=f32,
                )
                scores = jnp.where(same_item, scores, lowest)
                top = jnp.max(scores, axis=-1, keepdims=True)
                weight = jnp.exp2(scores - top).astype(bf16)
                denominator = jnp.sum(weight.astype(f32), axis=-1, keepdims=True)
                total = jnp.dot(
                    weight,
                    lines[:, 2 * attended + low : 2 * attended + low + HEAD_SIZE],
                    preferred_element_type=f32,
                )
                answer[:, rows, low : low + HEAD_SIZE] = (
                    (total / denominator).astype(bf16).reshape(peers, GROUP, HEAD_SIZE)
                )
            return inner

        lax.fori_loop(0, half_item // GROUP, group_step, 0)

        def send_step(step, inner):
            return_copy(me, lax.rem(me + step, peers), half).start()
            return inner

        lax.fori_loop(1, peers, send_step, 0)
        return carry

    lax.fori_loop(0, 2, half_step, 0)
    returned[me] = answer[me]
    loads[3].wait()

    velocity_rows = chunk // 8
    lane = lax.broadcasted_iota(jnp.int32, (chunk, LANES), 1)
    line = lax.broadcasted_iota(jnp.int32, (chunk, LANES), 0)
    keep = lane // (LANES // 8) == lax.rem(line, 8)

    def final_step(index, carry):
        pair = lax.rem(my_pair + index, pairs)
        for part in range(PAIR):
            source = pair * PAIR + part

            @pl.when(source != me)
            def _():
                return_copy(source, source, 0).wait_recv()
                return_copy(source, source, 1).wait_recv()

        rows = pl.ds(pl.multiple_of(pair * chunk, chunk), chunk)
        lines = returned[pl.ds(pair * PAIR, PAIR)].reshape(chunk, attended)
        product = jnp.dot(lines, temporal_out[...], preferred_element_type=f32)
        block = residual[rows, :] + gate * product
        hidden_out[rows, :] = block.astype(bf16)
        final_rows = (layer_norm(block) * gain[...]).astype(bf16)
        wide = times_turned(final_rows, wide_weight[...])
        packed = jnp.sum(jnp.where(keep, wide, 0.0).reshape(velocity_rows, 8, LANES), axis=1)
        velocity_out[pl.ds(pl.multiple_of(pair * velocity_rows, velocity_rows), velocity_rows), :] = (
            packed
        )
        return carry

    lax.fori_loop(0, pairs, final_step, 0)
    update_sent[...] = (latents[...] + time_delta * velocity_out[...]).astype(bf16)
    next_copy = pltpu.make_async_remote_copy(
        src_ref=update_sent,
        dst_ref=update_received,
        send_sem=next_send,
        recv_sem=next_recv,
        device_id={"frame": lax.rem(me + 1, peers)},
        device_id_type=MESH,
    )
    next_copy.start()

    def drain(index, carry):
        kv_copy(index).wait_send()
        return carry

    lax.fori_loop(0, tokens // ROWS, drain, 0)

    def drain_peer(step, carry):
        target = lax.rem(me + step, peers)
        forward_copy(me, target).wait_send()
        return_copy(me, target, 0).wait_send()
        return_copy(me, target, 1).wait_send()
        return carry

    lax.fori_loop(1, peers, drain_peer, 0)
    next_copy.wait()

    @pl.when(me == 0)
    def _():
        next_out[...] = noise[...]

    @pl.when(me != 0)
    def _():
        next_out[...] = update_received[...].astype(f32)


def body(
    hidden_in,
    latents,
    fresh_noise,
    level_index,
    time_table,
    frame_offset,
    mod_table,
    time_weight,
    spatial_qkv,
    spatial_out,
    temporal_qkv,
    temporal_out,
    final_gain,
    out_weight,
):
    tokens, width = hidden_in.shape[1:]
    attended = spatial_out.shape[0]
    head_count = attended // HEAD_SIZE
    peers = lax.axis_size("frame")
    item = tokens // peers
    fits = (
        peers % PAIR == 0
        and tokens % ROWS == 0
        and item % (2 * GROUP) == 0
        and head_count % 2 == 0
        and lax.axis_size("band") == 2
        and peers * GROUP <= LANES
        and out_weight.shape[1] * 8 == LANES
    )
    if not fits:
        return plain_body(
            hidden_in,
            latents,
            fresh_noise,
            level_index,
            time_table,
            frame_offset,
            mod_table,
            time_weight,
            spatial_qkv,
            spatial_out,
            temporal_qkv,
            temporal_out,
            final_gain,
            out_weight,
        )
    def frequency(half):
        steps = np.arange(half, dtype=np.float64)
        return np.exp(-math.log(10000.0) * steps / half).astype(np.float32)[None, :]

    bf16, f32 = jnp.bfloat16, jnp.float32
    vmem = pl.BlockSpec(memory_space=pltpu.VMEM)
    anywhere = pl.BlockSpec(memory_space=pl.ANY)
    steps = tokens // ROWS
    chunk = PAIR * item
    dma = pltpu.SemaphoreType.DMA
    latent_rows = latents.shape[1]
    hidden_out, velocity, next_latents = pl.pallas_call(
        functools.partial(block_kernel, peers, head_count),
        out_shape=(
            jax.ShapeDtypeStruct((tokens, width), bf16),
            jax.ShapeDtypeStruct((latent_rows, LANES), f32),
            jax.ShapeDtypeStruct((latent_rows, LANES), f32),
        ),
        in_specs=[vmem]
        + [pl.BlockSpec(memory_space=pltpu.SMEM), vmem, pl.BlockSpec(memory_space=pltpu.SMEM)]
        + [vmem] * 8
        + [anywhere] * 4,
        out_specs=(vmem, vmem, vmem),
        scratch_shapes=[
            pltpu.VMEM(spatial_qkv.shape[::-1], bf16),
            pltpu.VMEM(spatial_out.shape, bf16),
            pltpu.VMEM(temporal_qkv.shape[::-1], bf16),
            pltpu.VMEM(temporal_out.shape, bf16),
            pltpu.VMEM((tokens, width), bf16),
            pltpu.VMEM((tokens, 3 * attended), bf16),
            pltpu.VMEM((tokens, 3 * attended - attended // LANES * LANES), bf16),
            pltpu.VMEM((head_count, tokens, LANES), bf16),
            pltpu.VMEM((head_count, 2 * tokens, LANES), bf16),
            pltpu.VMEM((head_count, 2 * tokens, LANES), bf16),
            pltpu.VMEM((head_count, chunk, LANES), bf16),
            pltpu.VMEM((chunk, attended), bf16),
            pltpu.VMEM((1, 3 * width), f32),
            pltpu.VMEM((1, width), f32),
            pltpu.VMEM((1, width), f32),
            pltpu.VMEM((LANES, width), bf16),
            pltpu.VMEM((tokens, width), f32),
            pltpu.VMEM((peers, item, width), bf16),
            pltpu.VMEM((peers, item, width), bf16),
            pltpu.VMEM((peers, item, 3 * attended), bf16),
            pltpu.VMEM((peers, item, attended), bf16),
            pltpu.VMEM((peers, item, attended), bf16),
            pltpu.VMEM((latent_rows, LANES), bf16),
            pltpu.VMEM((latent_rows, LANES), bf16),
            dma((4,)),
            dma((steps,)),
            dma((steps,)),
            dma((peers,)),
            dma((peers,)),
            dma((peers, 2)),
            dma((peers, 2)),
            dma,
            dma,
        ],
        compiler_params=pltpu.CompilerParams(
            collective_id=0, has_side_effects=True, vmem_limit_bytes=63 * 1024 * 1024
        ),
        name="block",
    )(
        hidden_in[0],
        level_index,
        time_table,
        frame_offset,
        frequency(time_weight.shape[0] // 2),
        frequency(width // 2),
        mod_table,
        time_weight,
        final_gain,
        out_weight.T,
        latents[0],
        fresh_noise,
        spatial_qkv.T,
        spatial_out,
        temporal_qkv.T,
        temporal_out,
    )
    return (hidden_out[None], velocity[None], next_latents[None])


def solution(mesh):
    placed = (
        P(("groups", "frame"), "band", None),
        P(("groups", "frame"), "band", None),
        P(("groups", "band"), None),
        P(("groups", "frame")),
        P(),
        P("groups"),
        P(),
        P(),
        P(),
        P(),
        P(),
        P(),
        P(),
        P(),
    )
    return jax.shard_map(
        body,
        mesh=mesh,
        in_specs=placed,
        out_specs=(
            P(("groups", "frame"), "band", None),
            P(("groups", "frame"), "band", None),
            P(("groups", "frame"), "band", None),
        ),
        check_vma=False,
    )
```

```python
import functools
import math

import jax
import jax.numpy as jnp
import numpy as np
from jax import lax
from jax.experimental import pallas as pl
from jax.experimental.pallas import tpu as pltpu
from jax.sharding import PartitionSpec as P

HEAD_SIZE = 72


epsilon = 1e-06


def from_behind(value, axis, steps):
    count = lax.axis_size(axis)
    initial, last = (max(0, -steps), min(count, count - steps))
    return lax.ppermute(value, axis, [(source, source + steps) for source in range(initial, last)])


def layer_norm(values):
    average = jnp.mean(values, axis=-1, keepdims=True)
    centred = values - average
    variance = jnp.mean(centred * centred, axis=-1, keepdims=True)
    return centred * lax.rsqrt(variance + epsilon)


def sinusoid(position, feature_count, first_sine):
    half_width = feature_count // 2
    frequency = jnp.exp(-math.log(10000.0) * jnp.arange(half_width, dtype=jnp.float32) / half_width)
    angles = position.astype(jnp.float32)[:, None] * frequency[None, :]
    if first_sine:
        return jnp.concatenate([jnp.sin(angles), jnp.cos(angles)], axis=-1)
    return jnp.concatenate([jnp.cos(angles), jnp.sin(angles)], axis=-1)


def mix_frames(rows, head_count):
    frame_count = rows.shape[0]
    item_count = rows.shape[1]
    parted = rows.reshape(frame_count, item_count, 3, head_count, HEAD_SIZE)
    attention_scores = jnp.einsum(
        "fnhd,gnhd->nhfg", parted[:, :, 0], parted[:, :, 1], preferred_element_type=jnp.float32
    ) / math.sqrt(HEAD_SIZE)
    row_max = jnp.max(attention_scores, axis=-1, keepdims=True)
    attention_weight = jnp.exp(attention_scores - row_max).astype(jnp.bfloat16)
    denominator = jnp.sum(attention_weight, axis=-1, dtype=jnp.float32)
    weighted_sum = jnp.einsum(
        "nhfg,gnhd->fnhd", attention_weight, parted[:, :, 2], preferred_element_type=jnp.float32
    )
    mixed = weighted_sum / jnp.transpose(denominator, (2, 0, 1))[..., None]
    return mixed.astype(jnp.bfloat16).reshape(frame_count, item_count, head_count * HEAD_SIZE)


def plain_body(
    hidden_in,
    latents,
    fresh_noise,
    level_index,
    time_table,
    frame_offset,
    mod_table,
    time_weight,
    spatial_qkv,
    spatial_out,
    temporal_qkv,
    temporal_out,
    final_gain,
    out_weight,
):
    tokens = hidden_in.shape[1]
    model_width = hidden_in.shape[2]
    attended = spatial_out.shape[0]
    head_count = attended // HEAD_SIZE
    peers = lax.axis_size("frame")
    table_index = jnp.arange(time_table.shape[0], dtype=jnp.int32)
    now_steps = jnp.sum(
        jnp.where(table_index[None, :] == level_index[:, None], time_table[None, :], 0), axis=1
    )
    next_steps = jnp.sum(
        jnp.where(table_index[None, :] == level_index[:, None] - 1, time_table[None, :], 0), axis=1
    )
    activated = jax.nn.silu(sinusoid(now_steps, time_weight.shape[0], False)).astype(jnp.bfloat16)
    modulation = mod_table[None, :] + jnp.dot(
        activated, time_weight, preferred_element_type=jnp.float32
    )
    shift_part = modulation[:, :model_width]
    scale_part = modulation[:, model_width : 2 * model_width]
    gate_part = modulation[:, 2 * model_width :]
    inputs = hidden_in[0].astype(jnp.float32)
    normed = (layer_norm(inputs) * (1.0 + scale_part) + shift_part).astype(jnp.bfloat16)
    projected = jnp.dot(normed, spatial_qkv, preferred_element_type=jnp.float32).astype(
        jnp.bfloat16
    )
    query_rows = projected[:, :attended].reshape(tokens, head_count, HEAD_SIZE)
    key_value = projected[:, attended:]
    block_rows = lax.all_gather(key_value, "band", axis=0, tiled=True)
    row_max = jnp.full((head_count, tokens), -1e30, jnp.float32)
    row_count = block_rows.shape[0]
    key_matrix_rows = block_rows[:, :attended].reshape(row_count, head_count, HEAD_SIZE)
    value_matrix_rows = block_rows[:, attended:].reshape(row_count, head_count, HEAD_SIZE)
    attention_scores = jnp.einsum(
        "ubg,wbg->buw", query_rows, key_matrix_rows, preferred_element_type=jnp.float32
    ) / math.sqrt(HEAD_SIZE)
    new_max = jnp.maximum(row_max, jnp.max(attention_scores, axis=-1))
    attention_weight = jnp.exp(attention_scores - new_max[:, :, None]).astype(jnp.bfloat16)
    denominator = jnp.sum(attention_weight, axis=-1, dtype=jnp.float32)
    weighted_sum = jnp.einsum(
        "leq,qlr->ler", attention_weight, value_matrix_rows, preferred_element_type=jnp.float32
    )
    row_max, denominator, weighted_sum = (new_max, denominator, weighted_sum)
    spatial_mixed = (
        jnp.transpose(weighted_sum / denominator[:, :, None], (1, 0, 2))
        .reshape(tokens, attended)
        .astype(jnp.bfloat16)
    )
    residual = inputs + gate_part * jnp.dot(
        spatial_mixed, spatial_out, preferred_element_type=jnp.float32
    )
    position = lax.axis_index("frame") + frame_offset
    placed = sinusoid(position, model_width, True)
    temporal_in = (residual + placed).astype(jnp.bfloat16)
    spread_rows = temporal_in.reshape(1, peers, tokens // peers, model_width)
    gathered = lax.all_to_all(spread_rows, "frame", split_axis=1, concat_axis=0, tiled=True)
    frame_count = gathered.shape[0]
    item_count = gathered.shape[2]
    rows = jnp.dot(
        gathered.reshape(frame_count * item_count, model_width),
        temporal_qkv,
        preferred_element_type=jnp.float32,
    ).astype(jnp.bfloat16)
    mixed = mix_frames(rows.reshape(frame_count, item_count, 3 * attended), head_count)
    mixed_rows = mixed.reshape(frame_count, 1, item_count, attended)
    mixed_pairs = mixed_rows.reshape(mixed_rows.shape[0], 1, mixed_rows.shape[2] // 2, 2 * attended)
    returned = lax.all_to_all(mixed_pairs, "frame", split_axis=0, concat_axis=1, tiled=True)
    temporal_mixed = returned.reshape(tokens, attended)
    residual = residual + gate_part * jnp.dot(
        temporal_mixed, temporal_out, preferred_element_type=jnp.float32
    )
    hidden_out = residual.astype(jnp.bfloat16)[None]
    final_rows = (layer_norm(residual) * final_gain).astype(jnp.bfloat16)
    velocity = jnp.dot(final_rows, out_weight, preferred_element_type=jnp.float32).reshape(
        1, latents.shape[1], 128
    )
    time_delta = (next_steps - now_steps).astype(jnp.float32) / 1000.0
    update = latents + time_delta[:, None, None] * velocity
    shifted = from_behind(update.astype(jnp.bfloat16), "frame", 1).astype(update.dtype)
    next_latents = jnp.where(lax.axis_index("frame") == 0, fresh_noise[None], shifted)
    return (hidden_out, velocity, next_latents)


MESH = pl.DeviceIdType.MESH
ROWS = 256
PAIR = 2
GROUP = 16
LANES = 128


def times_turned(rows, turned):
    return lax.dot_general(
        rows, turned, (((1,), (1,)), ((), ())), preferred_element_type=jnp.float32
    )


def block_kernel(
    peers,
    head_count,
    hidden,
    level_index,
    time_table,
    frame_offset,
    time_frequency,
    place_frequency,
    mod_table,
    time_weight,
    final_gain,
    out_weight,
    latents,
    noise,
    spatial_qkv_hbm,
    spatial_out_hbm,
    temporal_qkv_hbm,
    temporal_out_hbm,
    hidden_out,
    velocity_out,
    next_out,
    spatial_qkv,
    spatial_out,
    temporal_qkv,
    temporal_out,
    normed,
    projected,
    remote_kv,
    query,
    key,
    value,
    head_out,
    mixed,
    mod,
    placed,
    gain,
    wide_weight,
    residual,
    outgoing,
    gathered,
    temporal,
    answer,
    returned,
    update_sent,
    update_received,
    far_hidden,
    far_mixed,
    far_gate,
    gate_sent,
    mixed_sent,
    early_send,
    early_recv,
    weight_sem,
    kv_send,
    kv_recv,
    fwd_send,
    fwd_recv,
    ret_send,
    ret_recv,
    next_send,
    next_recv,
):
    f32, bf16 = jnp.float32, jnp.bfloat16
    tokens, width = hidden.shape
    attended = head_count * HEAD_SIZE
    item = tokens // peers
    me = lax.axis_index("frame")
    mate = 1 - lax.axis_index("band")
    pairs = peers // PAIR
    my_pair = me // PAIR
    chunk = PAIR * item
    first_kv = attended // LANES * LANES
    kv_shift = attended - first_kv
    query_factor = math.log2(math.e) / math.sqrt(HEAD_SIZE)

    loads = [
        pltpu.make_async_copy(source, target, weight_sem.at[index])
        for index, (source, target) in enumerate(
            (
                (spatial_qkv_hbm, spatial_qkv),
                (spatial_out_hbm, spatial_out),
                (temporal_qkv_hbm, temporal_qkv),
                (temporal_out_hbm, temporal_out),
            )
        )
    ]
    for load in loads:
        load.start()

    barrier = pltpu.get_barrier_semaphore()
    pl.semaphore_signal(barrier, inc=1, device_id={"band": mate}, device_id_type=MESH)
    for step in range(1, peers):
        pl.semaphore_signal(
            barrier, inc=1, device_id={"frame": lax.rem(me + step, peers)}, device_id_type=MESH
        )

    table = time_table[...].reshape(1, time_table.shape[0]).astype(f32)
    entry = lax.broadcasted_iota(jnp.int32, table.shape, 1)
    level = level_index[0]
    now_step = jnp.sum(jnp.where(entry == level, table, 0.0), axis=1, keepdims=True)
    next_step = jnp.sum(jnp.where(entry == level - 1, table, 0.0), axis=1, keepdims=True)
    time_delta = (next_step - now_step) / 1000.0
    angles = now_step * time_frequency[...]
    activated = jax.nn.silu(jnp.concatenate([jnp.cos(angles), jnp.sin(angles)], axis=-1))
    mod[...] = mod_table[...].reshape(1, 3 * width) + jnp.dot(
        activated.astype(bf16), time_weight[...], preferred_element_type=f32
    )
    gate_sent[...] = mod[:, 2 * width :]

    def placement(frame):
        places = (frame + frame_offset[0]).astype(f32) * place_frequency[...]
        return jnp.concatenate([jnp.sin(places), jnp.cos(places)], axis=-1)

    placed[0:1, :] = placement(me)
    for part in range(PAIR):
        placed[part + 1 : part + 2, :] = placement(
            lax.rem(my_pair + pairs // 2, pairs) * PAIR + part
        )
    gain[...] = final_gain[...].reshape(1, width)
    for copy in range(8):
        wide_weight[copy * (LANES // 8) : (copy + 1) * (LANES // 8), :] = out_weight[...]
    column = lax.broadcasted_iota(jnp.int32, (1, 3 * attended), 1)
    column_factor = jnp.where(column < attended, query_factor, 1.0).astype(f32)
    gate = mod[:, 2 * width :]

    def norm_step(index, carry):
        rows = pl.ds(pl.multiple_of(index * 64, 64), 64)
        lines = layer_norm(hidden[rows, :].astype(f32))
        normed[rows, :] = (lines * (1.0 + mod[:, width : 2 * width]) + mod[:, :width]).astype(bf16)
        return carry

    lax.fori_loop(0, tokens // 64, norm_step, 0)
    for heads in (query, key):
        heads[:, :, HEAD_SIZE:] = jnp.zeros(heads.shape[:2] + (LANES - HEAD_SIZE,), bf16)
    value[:, :, HEAD_SIZE:] = jnp.ones(value.shape[:2] + (LANES - HEAD_SIZE,), bf16)
    pl.semaphore_wait(barrier, peers)
    far_pair = lax.rem(my_pair + pairs // 2, pairs)
    my_part = lax.rem(me, PAIR)

    def early_copies(part):
        target = far_pair * PAIR + part
        rows = pl.ds(pl.multiple_of(target * item, item), item)
        return [
            pltpu.make_async_remote_copy(
                src_ref=source,
                dst_ref=place,
                send_sem=early_send.at[part, kind],
                recv_sem=early_recv.at[my_part, kind],
                device_id={"frame": target},
                device_id_type=MESH,
            )
            for kind, (source, place) in enumerate(
                (
                    (gate_sent, far_gate.at[my_part]),
                    (hidden.at[rows, :], far_hidden.at[my_part]),
                    (mixed_sent.at[part], far_mixed.at[my_part]),
                )
            )
        ]

    def early_arrivals(part):
        return [
            pltpu.make_async_remote_copy(
                src_ref=place,
                dst_ref=place,
                send_sem=early_send.at[part, kind],
                recv_sem=early_recv.at[part, kind],
                device_id={"frame": far_pair * PAIR + part},
                device_id_type=MESH,
            )
            for kind, place in enumerate(
                (far_gate.at[part], far_hidden.at[part], far_mixed.at[part])
            )
        ]

    for part in range(PAIR):
        early_copies(part)[0].start()
        early_copies(part)[1].start()
    loads[0].wait()

    def kv_copy(index):
        rows = pl.ds(pl.multiple_of(index * ROWS, ROWS), ROWS)
        return pltpu.make_async_remote_copy(
            src_ref=projected.at[rows, pl.ds(first_kv, 3 * attended - first_kv)],
            dst_ref=remote_kv.at[rows, :],
            send_sem=kv_send.at[index],
            recv_sem=kv_recv.at[index],
            device_id={"band": mate},
            device_id_type=MESH,
        )

    def project_step(index, carry):
        rows = pl.ds(pl.multiple_of(index * ROWS, ROWS), ROWS)
        product = times_turned(normed[rows, :], spatial_qkv[...])
        projected[rows, :] = (product * column_factor).astype(bf16)
        kv_copy(index).start()
        return carry

    lax.fori_loop(0, tokens // ROWS, project_step, 0)

    def split_own(index, carry):
        rows = pl.ds(pl.multiple_of(index * ROWS, ROWS), ROWS)
        for head in range(head_count):
            low = head * HEAD_SIZE
            query[head, rows, :HEAD_SIZE] = projected[rows, low : low + HEAD_SIZE]
            low += attended
            key[head, rows, :HEAD_SIZE] = projected[rows, low : low + HEAD_SIZE]
            low += attended
            value[head, rows, :HEAD_SIZE] = projected[rows, low : low + HEAD_SIZE]
        return carry

    lax.fori_loop(0, tokens // ROWS, split_own, 0)

    def split_remote(index, carry):
        kv_copy(index).wait_recv()
        rows = pl.ds(pl.multiple_of(index * ROWS, ROWS), ROWS)
        there = pl.ds(pl.multiple_of(tokens + index * ROWS, ROWS), ROWS)
        for head in range(head_count):
            low = head * HEAD_SIZE + kv_shift
            key[head, there, :HEAD_SIZE] = remote_kv[rows, low : low + HEAD_SIZE]
            low += attended
            value[head, there, :HEAD_SIZE] = remote_kv[rows, low : low + HEAD_SIZE]
        return carry

    lax.fori_loop(0, tokens // ROWS, split_remote, 0)
    loads[1].wait()

    def forward_copy(source, target):
        return pltpu.make_async_remote_copy(
            src_ref=outgoing.at[target],
            dst_ref=gathered.at[source],
            send_sem=fwd_send.at[target],
            recv_sem=fwd_recv.at[source],
            device_id={"frame": target},
            device_id_type=MESH,
        )

    def query_step(index, carry):
        pair = lax.rem(my_pair + 1 + index, pairs)
        rows = pl.ds(pl.multiple_of(pair * chunk, chunk), chunk)

        def head_step(half, inner):
            for part in range(2):
                head = half * 2 + part
                scores = lax.dot_general(
                    query[head, rows, :],
                    key[head],
                    (((1,), (1,)), ((), ())),
                    preferred_element_type=f32,
                )
                top = jnp.max(scores, axis=-1, keepdims=True)
                weight = jnp.exp2(scores - top).astype(bf16)
                total = jnp.dot(weight, value[head], preferred_element_type=f32)
                head_out[head] = (total / total[:, HEAD_SIZE : HEAD_SIZE + 1]).astype(bf16)
            return inner

        lax.fori_loop(0, head_count // 2, head_step, 0)
        for head in range(head_count):
            mixed[:, head * HEAD_SIZE : (head + 1) * HEAD_SIZE] = head_out[head, :, :HEAD_SIZE]
        product = jnp.dot(mixed[...], spatial_out[...], preferred_element_type=f32)
        lines = hidden[rows, :].astype(f32) + gate * product
        residual[rows, :] = lines
        sent = (lines + placed[0:1, :]).astype(bf16)

        @pl.when(pair == far_pair)
        def _():
            for part in range(PAIR):
                mixed_sent[part] = mixed[part * item : (part + 1) * item, :]
                early_copies(part)[2].start()

        @pl.when(pair != far_pair)
        def _():
            for part in range(PAIR):
                outgoing[pair * PAIR + part] = sent[part * item : (part + 1) * item]
            for part in range(PAIR):
                target = pair * PAIR + part

                @pl.when(target != me)
                def _():
                    forward_copy(me, target).start()

        @pl.when(pair == my_pair)
        def _():
            for part in range(PAIR):

                @pl.when(my_part == part)
                def _():
                    gathered[me] = sent[part * item : (part + 1) * item]

        return carry

    lax.fori_loop(0, pairs, query_step, 0)
    loads[2].wait()

    def temporal_step(index, carry):
        pair = lax.rem(my_pair + 2 * pairs - 1 - index, pairs)
        @pl.when(pair == far_pair)
        def _():
            for part in range(PAIR):
                for copy in early_arrivals(part):
                    copy.wait_recv()
            product = jnp.dot(
                far_mixed[...].reshape(chunk, attended), spatial_out[...], preferred_element_type=f32
            )
            for part in range(PAIR):
                lines = far_hidden[part].astype(f32) + (
                    far_gate[part] * product[part * item : (part + 1) * item]
                )
                gathered[far_pair * PAIR + part] = (
                    lines + placed[part + 1 : part + 2, :]
                ).astype(bf16)

        @pl.when(pair != far_pair)
        def _():
            for part in range(PAIR):
                source = pair * PAIR + part

                @pl.when(source != me)
                def _():
                    forward_copy(source, source).wait_recv()

        lines = gathered[pl.ds(pair * PAIR, PAIR)].reshape(chunk, width)
        product = times_turned(lines, temporal_qkv[...])
        temporal[pl.ds(pair * PAIR, PAIR)] = (
            (product * column_factor).astype(bf16).reshape(PAIR, item, 3 * attended)
        )
        return carry

    lax.fori_loop(0, pairs, temporal_step, 0)

    count = peers * GROUP
    row_item = lax.rem(lax.broadcasted_iota(jnp.int32, (count, count), 0), GROUP)
    column_item = lax.rem(lax.broadcasted_iota(jnp.int32, (count, count), 1), GROUP)
    same_item = row_item == column_item
    lowest = float(jnp.finfo(f32).min)
    groups = item // GROUP
    ones = jnp.ones((count, HEAD_SIZE), bf16)

    def return_copy(source, target, group):
        rows = pl.ds(pl.multiple_of(group * GROUP, GROUP), GROUP)
        return pltpu.make_async_remote_copy(
            src_ref=answer.at[target, rows, :],
            dst_ref=returned.at[source, rows, :],
            send_sem=ret_send.at[target, group],
            recv_sem=ret_recv.at[source, group],
            device_id={"frame": target},
            device_id_type=MESH,
        )

    def group_step(group, carry):
        rows = pl.ds(pl.multiple_of(group * GROUP, GROUP), GROUP)
        lines = temporal[:, rows, :].reshape(count, 3 * attended)
        for head in range(head_count):
            low = head * HEAD_SIZE
            scores = lax.dot_general(
                lines[:, low : low + HEAD_SIZE],
                lines[:, attended + low : attended + low + HEAD_SIZE],
                (((1,), (1,)), ((), ())),
                preferred_element_type=f32,
            )
            scores = jnp.where(same_item, scores, lowest)
            top = jnp.max(scores, axis=-1, keepdims=True)
            weight = jnp.exp2(scores - top).astype(bf16)
            denominator = jnp.dot(weight, ones, preferred_element_type=f32)
            total = jnp.dot(
                weight,
                lines[:, 2 * attended + low : 2 * attended + low + HEAD_SIZE],
                preferred_element_type=f32,
            )
            answer[:, rows, low : low + HEAD_SIZE] = (
                (total / denominator).astype(bf16).reshape(peers, GROUP, HEAD_SIZE)
            )

        def send_step(step, inner):
            return_copy(me, lax.rem(me + step, peers), group).start()
            return inner

        lax.fori_loop(1, peers, send_step, 0)
        return carry

    lax.fori_loop(0, groups, group_step, 0)
    returned[me] = answer[me]
    loads[3].wait()

    velocity_rows = chunk // 8
    lane = lax.broadcasted_iota(jnp.int32, (chunk, LANES), 1)
    line = lax.broadcasted_iota(jnp.int32, (chunk, LANES), 0)
    keep = lane // (LANES // 8) == lax.rem(line, 8)

    def final_step(index, carry):
        pair = lax.rem(my_pair + index, pairs)
        for part in range(PAIR):
            source = pair * PAIR + part

            @pl.when(source != me)
            def _():
                for group in range(groups):
                    return_copy(source, source, group).wait_recv()

        rows = pl.ds(pl.multiple_of(pair * chunk, chunk), chunk)
        lines = returned[pl.ds(pair * PAIR, PAIR)].reshape(chunk, attended)
        product = jnp.dot(lines, temporal_out[...], preferred_element_type=f32)
        block = residual[rows, :] + gate * product
        hidden_out[rows, :] = block.astype(bf16)
        final_rows = (layer_norm(block) * gain[...]).astype(bf16)
        wide = times_turned(final_rows, wide_weight[...])
        packed = jnp.sum(jnp.where(keep, wide, 0.0).reshape(velocity_rows, 8, LANES), axis=1)
        velocity_out[pl.ds(pl.multiple_of(pair * velocity_rows, velocity_rows), velocity_rows), :] = (
            packed
        )
        return carry

    lax.fori_loop(0, pairs, final_step, 0)
    update_sent[...] = (latents[...] + time_delta * velocity_out[...]).astype(bf16)
    next_copy = pltpu.make_async_remote_copy(
        src_ref=update_sent,
        dst_ref=update_received,
        send_sem=next_send,
        recv_sem=next_recv,
        device_id={"frame": lax.rem(me + 1, peers)},
        device_id_type=MESH,
    )
    next_copy.start()

    def drain(index, carry):
        kv_copy(index).wait_send()
        return carry

    lax.fori_loop(0, tokens // ROWS, drain, 0)

    def drain_peer(step, carry):
        target = lax.rem(me + step, peers)

        @pl.when(target // PAIR != far_pair)
        def _():
            forward_copy(me, target).wait_send()

        for group in range(groups):
            return_copy(me, target, group).wait_send()
        return carry

    lax.fori_loop(1, peers, drain_peer, 0)
    for part in range(PAIR):
        for copy in early_copies(part):
            copy.wait_send()
    next_copy.wait()

    @pl.when(me == 0)
    def _():
        next_out[...] = noise[...]

    @pl.when(me != 0)
    def _():
        next_out[...] = update_received[...].astype(f32)


def body(
    hidden_in,
    latents,
    fresh_noise,
    level_index,
    time_table,
    frame_offset,
    mod_table,
    time_weight,
    spatial_qkv,
    spatial_out,
    temporal_qkv,
    temporal_out,
    final_gain,
    out_weight,
):
    tokens, width = hidden_in.shape[1:]
    attended = spatial_out.shape[0]
    head_count = attended // HEAD_SIZE
    peers = lax.axis_size("frame")
    item = tokens // peers
    fits = (
        peers % (2 * PAIR) == 0
        and tokens % ROWS == 0
        and item % (2 * GROUP) == 0
        and head_count % 2 == 0
        and lax.axis_size("band") == 2
        and peers * GROUP <= LANES
        and out_weight.shape[1] * 8 == LANES
    )
    if not fits:
        return plain_body(
            hidden_in,
            latents,
            fresh_noise,
            level_index,
            time_table,
            frame_offset,
            mod_table,
            time_weight,
            spatial_qkv,
            spatial_out,
            temporal_qkv,
            temporal_out,
            final_gain,
            out_weight,
        )
    def frequency(half):
        steps = np.arange(half, dtype=np.float64)
        return np.exp(-math.log(10000.0) * steps / half).astype(np.float32)[None, :]

    bf16, f32 = jnp.bfloat16, jnp.float32
    vmem = pl.BlockSpec(memory_space=pltpu.VMEM)
    anywhere = pl.BlockSpec(memory_space=pl.ANY)
    steps = tokens // ROWS
    chunk = PAIR * item
    dma = pltpu.SemaphoreType.DMA
    latent_rows = latents.shape[1]
    hidden_out, velocity, next_latents = pl.pallas_call(
        functools.partial(block_kernel, peers, head_count),
        out_shape=(
            jax.ShapeDtypeStruct((tokens, width), bf16),
            jax.ShapeDtypeStruct((latent_rows, LANES), f32),
            jax.ShapeDtypeStruct((latent_rows, LANES), f32),
        ),
        in_specs=[vmem]
        + [pl.BlockSpec(memory_space=pltpu.SMEM), vmem, pl.BlockSpec(memory_space=pltpu.SMEM)]
        + [vmem] * 8
        + [anywhere] * 4,
        out_specs=(vmem, vmem, vmem),
        scratch_shapes=[
            pltpu.VMEM(spatial_qkv.shape[::-1], bf16),
            pltpu.VMEM(spatial_out.shape, bf16),
            pltpu.VMEM(temporal_qkv.shape[::-1], bf16),
            pltpu.VMEM(temporal_out.shape, bf16),
            pltpu.VMEM((tokens, width), bf16),
            pltpu.VMEM((tokens, 3 * attended), bf16),
            pltpu.VMEM((tokens, 3 * attended - attended // LANES * LANES), bf16),
            pltpu.VMEM((head_count, tokens, LANES), bf16),
            pltpu.VMEM((head_count, 2 * tokens, LANES), bf16),
            pltpu.VMEM((head_count, 2 * tokens, LANES), bf16),
            pltpu.VMEM((head_count, chunk, LANES), bf16),
            pltpu.VMEM((chunk, attended), bf16),
            pltpu.VMEM((1, 3 * width), f32),
            pltpu.VMEM((8, width), f32),
            pltpu.VMEM((1, width), f32),
            pltpu.VMEM((LANES, width), bf16),
            pltpu.VMEM((tokens, width), f32),
            pltpu.VMEM((peers, item, width), bf16),
            pltpu.VMEM((peers, item, width), bf16),
            pltpu.VMEM((peers, item, 3 * attended), bf16),
            pltpu.VMEM((peers, item, attended), bf16),
            pltpu.VMEM((peers, item, attended), bf16),
            pltpu.VMEM((latent_rows, LANES), bf16),
            pltpu.VMEM((latent_rows, LANES), bf16),
            pltpu.VMEM((PAIR, item, width), bf16),
            pltpu.VMEM((PAIR, item, attended), bf16),
            pltpu.VMEM((PAIR, 1, width), f32),
            pltpu.VMEM((1, width), f32),
            pltpu.VMEM((PAIR, item, attended), bf16),
            dma((PAIR, 3)),
            dma((PAIR, 3)),
            dma((4,)),
            dma((steps,)),
            dma((steps,)),
            dma((peers,)),
            dma((peers,)),
            dma((peers, item // GROUP)),
            dma((peers, item // GROUP)),
            dma,
            dma,
        ],
        compiler_params=pltpu.CompilerParams(
            collective_id=0, has_side_effects=True, vmem_limit_bytes=63 * 1024 * 1024
        ),
        name="block",
    )(
        hidden_in[0],
        level_index,
        time_table,
        frame_offset,
        frequency(time_weight.shape[0] // 2),
        frequency(width // 2),
        mod_table,
        time_weight,
        final_gain,
        out_weight.T,
        latents[0],
        fresh_noise,
        spatial_qkv.T,
        spatial_out,
        temporal_qkv.T,
        temporal_out,
    )
    return (hidden_out[None], velocity[None], next_latents[None])


def solution(mesh):
    placed = (
        P(("groups", "frame"), "band", None),
        P(("groups", "frame"), "band", None),
        P(("groups", "band"), None),
        P(("groups", "frame")),
        P(),
        P("groups"),
        P(),
        P(),
        P(),
        P(),
        P(),
        P(),
        P(),
        P(),
    )
    return jax.shard_map(
        body,
        mesh=mesh,
        in_specs=placed,
        out_specs=(
            P(("groups", "frame"), "band", None),
            P(("groups", "frame"), "band", None),
            P(("groups", "frame"), "band", None),
        ),
        check_vma=False,
    )
```
